32 devices in a mesh: dp: 8 (over z, y), query: 4 (over x, core).
Axes of the slice: x: 2, y: 2, z: 4, core: 2. Of those that a mesh axis runs over, the one named last changes fastest.
Arguments:
- activations: bfloat16 [4096, 8192], P('dp', 'query'), may hold values from -6 to 6
- grads: bfloat16 [4096, 14336], P('dp', 'query'), may hold values from -6 to 6
- v_factors: bfloat16 [8192, 4096], P('query', 'dp'), may hold values from -0.0625 to 0.0625
- u_factors: bfloat16 [14336, 4096], P('query', 'dp'), may hold values from -0.001953125 to 0.001953125
- candidates: int32 [256, 2], P('dp'), may hold values from 0 to 7, all different within a row; in each aligned block of 32 rows (0 to 31, 32 to 63, ...) at most 16 rows name the same one
Outputs:
- scores: float32 [256, 2, 16], P('dp', None, 'query')
The draws below stay inside these ranges and needn't reach their ends.
Inputs may be any that keep to these rules, and one draw needn't show every extreme that they name: `candidates`: each row names 2 different query blocks. Among the 32 rows of one index of dp, no query block is named more than 16 times.
All inputs are finite; a program needn't handle non-finite values.
Results may differ from the reference program's by a relative error of at most 0.0003.
Values may be sent and summed in bfloat16 or wider, within the bound.
No kernel may reach another device: no remote copies, remote signals or barrier semaphores. Data moves between devices by JAX's collectives and lax.ppermute only.
A program may use at most 128 MiB of HBM per device.

```python
import math
import jax
import jax.numpy as jnp
import numpy as np
from jax import lax

D = 8192
F = 14336
R = 32
TB = 16
QB = 16
CAND = 2
TBD = 32
CAP = 16
TRAIN_BLOCKS = 256
TOKENS = 4096
QUERIES = 128
N_DP = 8


def shard_levels(own_key, extent, shards, low, high):
    def one(position, parts):
        draws = jax.random.uniform(jax.random.fold_in(jax.random.fold_in(own_key, 6), position), (parts,), jnp.float32, low / len(shards), high / len(shards))
        return jnp.repeat(jnp.exp(draws), extent[position] // parts).reshape((-1,) + (1,) * (len(extent) - position - 1))

    level = one(*shards[0])
    for cut in shards[1:]:
        level = level * one(*cut)
    return level


def shared_out(rng, own, number, rows, number_of, top, bound, slope):
    order = jax.random.permutation(rng, number_of)
    crowded, usual = load_shares(number_of, rows * top, bound, slope, True), load_shares(number_of, rows * top, bound, slope, False)
    places = jnp.arange(number_of)

    def named(tallies, rotation):
        used = int((tallies > 0).sum())
        fixed = max(1, used // 4)
        moved = fixed + (places - fixed + rotation * (used - fixed)) % max(1, number_of - fixed)
        return jnp.zeros((number_of,), jnp.int32).at[order[jnp.where(places < fixed, places, moved)]].set(jnp.asarray(tallies, jnp.int32))

    tallies = jnp.where(number % 4 == 0, named(crowded, number // 4), named(usual, number - number // 4 - 1))
    mixed = jax.random.permutation(jax.random.fold_in(own, 3), number_of)
    giver, sink = mixed[0:number_of // 2 * 2:2], mixed[1:number_of // 2 * 2:2]
    margin = jnp.minimum(tallies[giver] - 1, bound - tallies[sink]) // 2
    margin = jnp.where((giver == order[0]) | (sink == order[0]) | (tallies[sink] == 0), 0, jnp.maximum(margin, 0))
    moved = jax.random.randint(jax.random.fold_in(own, 4), (number_of // 2,), 0, 1 << 20) % (margin + 1)
    tallies = tallies.at[giver].add(-moved).at[sink].add(moved)
    labels = jnp.searchsorted(jnp.cumsum(tallies), jnp.arange(rows * top), side="right").astype(jnp.int32)
    table = labels.reshape(top, rows).T
    table = table[jax.random.permutation(jax.random.fold_in(own, 1), rows)]
    rotation = jax.random.randint(jax.random.fold_in(own, 2), (rows, 1), 0, top)
    return jnp.take_along_axis(table, (jnp.arange(top)[None, :] + rotation) % top, axis=1)


def load_shares(count, total, reach, lean, full):
    weights = [(1 << 20) // math.isqrt(grade ** lean) + 1 for grade in range(1, count + 1)]
    largest = reach if full else min(reach, max(-(-total // count), total * weights[0] // sum(weights)))
    least = 1 if total - largest >= count - 1 else 0
    given, rest = [largest] + [least] * (count - 1), total - largest - least * (count - 1)
    while rest > 0:
        free = [i for i in range(1, count) if given[i] < largest] or [i for i in range(1, count) if given[i] < reach]
        whole, left = sum([weights[i] for i in free]), rest
        for i in free:
            more = min(reach - given[i], max(1, left * weights[i] // whole), rest)
            given[i] = given[i] + more
            rest = rest - more
    return np.array(given)


def bell_draw(key, dims, deviation, limit, shards=(), kind=jnp.bfloat16):
    values = jax.random.normal(key, dims, jnp.float32) * deviation
    if len(shards) > 0:
        values = shard_levels(key, dims, shards, -0.22, 0.18) * values
    return jnp.clip(values, min=-limit, max=limit).astype(kind)


def setup_inputs(seed: int = 0) -> dict:
    splits = jax.random.split(jax.random.key(seed), 6)
    activations = bell_draw(splits[0], (TOKENS, D), 1.0, 6.0, ((0, 8), (1, 4)))
    grads = bell_draw(splits[1], (TOKENS, F), 1.0, 6.0, ((0, 8), (1, 4)))
    v_factors = bell_draw(splits[2], (D, QUERIES * R), D ** -0.5, 0.0625, ((0, 4), (1, 8)))
    u_factors = bell_draw(splits[3], (F, QUERIES * R), (F * TB * R) ** -0.5, 0.001953125, ((0, 4), (1, 8)))
    candidates_keys = jax.random.split(jax.random.fold_in(splits[4], 1), TRAIN_BLOCKS // TBD)
    candidates_turns = jax.random.permutation(jax.random.fold_in(splits[4], 3), TRAIN_BLOCKS // TBD)
    candidates = jax.vmap(lambda own, number: shared_out(jax.random.fold_in(splits[4], 2), own, number, TBD, N_DP, CAND, CAP, 2))(candidates_keys, candidates_turns).reshape((TRAIN_BLOCKS, CAND))
    return {"activations": activations, "grads": grads, "v_factors": v_factors, "u_factors": u_factors, "candidates": candidates}


def reference(activations, grads, v_factors, u_factors, candidates):
    column_width = QB * R
    act_blocks = activations.reshape(TRAIN_BLOCKS, TB, D)
    grad_blocks = grads.reshape(TRAIN_BLOCKS, TB, F)

    def one_block(packed):
        act_rows, grad_rows, pairings = packed

        def one_pair(target):
            first_col = (target * column_width).astype(jnp.int32)
            v_cols = lax.dynamic_slice_in_dim(v_factors, first_col, column_width, 1)
            u_cols = lax.dynamic_slice_in_dim(u_factors, first_col, column_width, 1)
            proj_act = jnp.dot(act_rows, v_cols, preferred_element_type=jnp.float32)
            proj_grad = jnp.dot(grad_rows, u_cols, preferred_element_type=jnp.float32)
            products = (proj_act * proj_grad).reshape(TB, QB, R)
            return jnp.sum(products, axis=(0, 2))

        return lax.map(one_pair, pairings)

    return lax.map(one_block, (act_blocks, grad_blocks, candidates))
```

```python
import jax
import jax.numpy as jnp
from jax import lax
from jax.experimental import pallas as pl
from jax.experimental.pallas import tpu as pltpu
from jax.sharding import PartitionSpec as P

R = 32
TOKENS_PER_BLOCK = 16
VMEM_BYTES = 64 * 2**20


def local_scores(received, v_factors, u_factors, reducer):
    recv_act, recv_grad = received
    peer_total, item_count, token_count, width_act = recv_act.shape
    row_total = peer_total * item_count * token_count
    flat_act = recv_act.reshape(row_total, width_act)
    flat_grad = recv_grad.reshape(row_total, recv_grad.shape[3])

    def partial_term(first_row, row_count):
        proj_act = lax.dot_general(
            v_factors, flat_act, (((0,), (1,)), ((), ())), preferred_element_type=jnp.float32
        )
        proj_grad = lax.dot_general(
            u_factors, flat_grad, (((0,), (1,)), ((), ())), preferred_element_type=jnp.float32
        )
        return jnp.stack([proj_act, proj_grad], axis=1)

    reduced = reducer(partial_term)
    products = reduced[:, 0] * reduced[:, 1]
    local_queries = products.shape[0] // R
    summed = jnp.sum(
        products.reshape(local_queries, R, peer_total, item_count, token_count), axis=(1, 4)
    )
    return jnp.transpose(summed, (1, 2, 0))


def exchange_plan(activations, grads, v_factors, u_factors, candidates):
    peer_total = lax.axis_size("dp")
    blocks = candidates.shape[0]
    pick_count = candidates.shape[1]
    token_count = activations.shape[0] // blocks
    capacity = 2 * blocks * pick_count // peer_total
    width_act = activations.shape[1]
    width_grad = grads.shape[1]
    column_total = v_factors.shape[1]
    local_rows = column_total // lax.axis_size("query")
    entry_total = blocks * pick_count
    slot_total = peer_total * capacity
    target = candidates.reshape(entry_total)
    onehot = (target[:, None] == jnp.arange(peer_total, dtype=jnp.int32)[None, :]).astype(jnp.int32)
    earlier = jnp.cumsum(onehot, axis=0) - onehot
    slot_index = jnp.sum(earlier * onehot, axis=1)
    position = target * capacity + slot_index
    matches = (position[None, :] == jnp.arange(slot_total, dtype=jnp.int32)[:, None]).astype(
        jnp.int32
    )
    owner_block = jnp.arange(entry_total, dtype=jnp.int32) // pick_count
    source = jnp.sum(matches * owner_block[None, :], axis=1)
    filled = jnp.sum(matches, axis=1) > 0
    act_blocks = activations.reshape(blocks, token_count, width_act)
    grad_blocks = grads.reshape(blocks, token_count, width_grad)
    send_act = jnp.where(
        filled[:, None, None],
        jnp.take(act_blocks, source, axis=0),
        jnp.zeros((), activations.dtype),
    )
    send_grad = jnp.where(
        filled[:, None, None], jnp.take(grad_blocks, source, axis=0), jnp.zeros((), grads.dtype)
    )
    send_act = send_act.reshape(peer_total, capacity, token_count, width_act)
    send_grad = send_grad.reshape(peer_total, capacity, token_count, width_grad)
    scored = local_scores(
        (
            lax.all_to_all(send_act, "dp", split_axis=0, concat_axis=0, tiled=True),
            lax.all_to_all(send_grad, "dp", split_axis=0, concat_axis=0, tiled=True),
        ),
        v_factors,
        u_factors,
        lambda partial_term: lax.psum_scatter(
            partial_term(jnp.int32(0), local_rows * lax.axis_size("query")),
            "query",
            scatter_dimension=0,
            tiled=True,
        ),
    )
    returned = lax.all_to_all(scored, "dp", split_axis=0, concat_axis=0, tiled=True)
    flattened = returned.reshape(slot_total, returned.shape[2])
    picked = jnp.take(flattened, position, axis=0)
    return picked.reshape(blocks, pick_count, returned.shape[2])


def swap_pairs(total, mask):
    return [(index, index ^ mask) for index in range(total)]


def projections(units, sources, factors, order, core, after=()):
    count = len(units)
    capacity = order.shape[1]
    width, columns = factors[0].shape
    token_count = TOKENS_PER_BLOCK
    rows = capacity * token_count
    quarter = columns // 4

    def body(order_ref, core_ref, *refs):
        source_refs = refs[: len(sources)]
        factor_refs = refs[len(sources) : len(sources) + len(factors)]
        middle = core_ref[1] == 1
        keep_ref, send_ref, token_buffer, factor_buffer, token_done, factor_done = refs[-6:]

        def factor_copy(which):
            return pltpu.make_async_copy(
                factor_refs[which], factor_buffer.at[which], factor_done.at[which]
            )

        started = set()
        for unit, (source, factor, first) in enumerate(units):

            def gather(origin, unit=unit, first=first):
                for slot in range(capacity):
                    block = order_ref[first, slot]
                    pltpu.make_async_copy(
                        origin.at[pl.ds(block * token_count, token_count)],
                        token_buffer.at[unit, pl.ds(slot * token_count, token_count)],
                        token_done.at[unit],
                    ).start()

            if source == 0:
                gather(source_refs[0])
            else:
                pl.when(middle)(lambda: gather(source_refs[1]))
                pl.when(jnp.logical_not(middle))(lambda: gather(source_refs[2]))
            if factor not in started:
                started.add(factor)
                factor_copy(factor).start()
        waited = set()
        for unit, (source, factor, first) in enumerate(units):
            pltpu.make_async_copy(
                source_refs[0].at[pl.ds(0, rows)], token_buffer.at[unit], token_done.at[unit]
            ).wait()
            if factor not in waited:
                waited.add(factor)
                factor_copy(factor).wait()
            product = jnp.dot(
                token_buffer[unit], factor_buffer[factor], preferred_element_type=jnp.float32
            )
            span = pl.ds(unit * rows, rows)
            parts = [product[:, place * quarter : (place + 1) * quarter] for place in range(4)]
            first_core = core_ref[0] == 0
            for side in range(2):
                keep_ref[side, span] = jnp.where(first_core, parts[2 * side], parts[2 * side + 1])
                send_ref[side, span] = jnp.where(first_core, parts[2 * side + 1], parts[2 * side])

    anywhere = pl.BlockSpec(memory_space=pltpu.HBM)
    scalars = pl.BlockSpec(memory_space=pltpu.SMEM)
    result = jax.ShapeDtypeStruct((2, count * rows, quarter), jnp.float32)
    return pl.pallas_call(
        body,
        out_shape=(result, result),
        in_specs=[scalars, scalars] + [anywhere] * (len(sources) + len(factors) + len(after)),
        scratch_shapes=[
            pltpu.VMEM((count, rows, width), sources[0].dtype),
            pltpu.VMEM((len(factors), width, columns), factors[0].dtype),
            pltpu.SemaphoreType.DMA((count,)),
            pltpu.SemaphoreType.DMA((len(factors),)),
        ],
        compiler_params=pltpu.CompilerParams(vmem_limit_bytes=VMEM_BYTES),
    )(order, core, *sources, *factors, *after)


def block_scores(acts, gradients, side, positions):
    rows, quarter = acts[2].shape
    slots = rows // TOKENS_PER_BLOCK
    queries = quarter // R
    entries = positions[0].shape[0]
    outputs = len(positions)

    def body(side_ref, *refs):
        keep_a, came_a, far_a, keep_g, came_g, far_g = (ref[...].reshape(rows, quarter) for ref in refs[:6])
        products = (keep_a + came_a + far_a) * (keep_g + came_g + far_g)
        per_slot = jnp.sum(products.reshape(slots, TOKENS_PER_BLOCK, quarter), axis=1)
        lane = lax.broadcasted_iota(jnp.int32, (quarter, queries), 0)
        query = lax.broadcasted_iota(jnp.int32, (quarter, queries), 1)
        groups = jnp.where(lane // R == query, 1.0, 0.0).astype(jnp.float32)
        sums = jnp.dot(
            per_slot, groups, precision=lax.Precision.HIGHEST, preferred_element_type=jnp.float32
        )
        for position_ref, out_ref in zip(refs[6 : 6 + outputs], refs[6 + outputs :]):
            slot = lax.broadcasted_iota(jnp.int32, (entries, slots), 1)
            chosen = jnp.where(position_ref[...] == slot, 1.0, 0.0).astype(jnp.float32)
            out_ref[...] = jnp.dot(
                chosen, sums, precision=lax.Precision.HIGHEST, preferred_element_type=jnp.float32
            )

    half = pl.BlockSpec((1, rows, quarter), lambda step, side_ref: (side_ref[0], 0, 0))
    whole = pl.BlockSpec((rows, quarter), lambda step, side_ref: (0, 0))
    placed = pl.BlockSpec((entries, 1), lambda step, side_ref: (0, 0))
    given = pl.BlockSpec((entries, queries), lambda step, side_ref: (0, 0))
    return pl.pallas_call(
        body,
        out_shape=(jax.ShapeDtypeStruct((entries, queries), jnp.float32),) * outputs,
        grid_spec=pltpu.PrefetchScalarGridSpec(
            num_scalar_prefetch=1,
            grid=(1,),
            in_specs=[half, half, whole] * 2 + [placed] * outputs,
            out_specs=(given,) * outputs,
        ),
    )(side, *acts, *gradients, *positions)


def slots_of(named, me, capacity):
    blocks, pick_count = named.shape
    entries = blocks * pick_count
    relative = (named ^ me).reshape(entries)
    onehot = (relative[:, None] == jnp.arange(4, dtype=jnp.int32)[None, :]).astype(jnp.int32)
    earlier = jnp.cumsum(onehot, axis=0) - onehot
    position = relative * capacity + jnp.sum(earlier * onehot, axis=1)
    position = jnp.where(relative < 4, position, -1)
    matches = position[None, :] == jnp.arange(4 * capacity, dtype=jnp.int32)[:, None]
    owner = jnp.arange(entries, dtype=jnp.int32) // pick_count
    order = jnp.sum(jnp.where(matches, owner[None, :], 0), axis=1)
    return order.reshape(4, capacity), position.reshape(entries, 1)


def mirror_plan(activations, grads, v_factors, u_factors, candidates):
    me = lax.axis_index("dp")
    place = lax.axis_index("query")
    side = (place // 2).reshape(1)
    blocks, pick_count = candidates.shape
    capacity = 2 * blocks * pick_count // 8
    across_z = swap_pairs(8, 2)
    across_y = swap_pairs(8, 1)
    mirror = swap_pairs(8, 6)
    inner = mirror[2:6]
    outer = mirror[:2] + mirror[6:]
    is_inner = jnp.logical_and(me >= 2, me < 6).astype(jnp.int32)
    core = jnp.stack([place % 2, is_inner])

    def swap(array, pairs):
        return lax.ppermute(array, "dp", pairs)

    mirrored = swap(candidates, mirror)
    u_y = swap(u_factors, across_y)
    u_z = swap(u_factors, across_z)
    v_y = swap(v_factors, across_y)
    v_z = swap(v_factors, across_z)
    g_in = swap(grads, inner)
    a_in = swap(activations, inner)
    g_out = swap(grads, outer)
    a_out = swap(activations, outer)
    u_d = swap(u_z, across_y)
    v_d = swap(v_z, across_y)

    near_order, near_position = slots_of(candidates, me, capacity)
    far_order, far_position = slots_of(mirrored, me, capacity)
    order = jnp.concatenate([near_order, far_order], axis=0)

    def reduced(halves):
        keep, send = halves
        came = lax.ppermute(send, "query", swap_pairs(4, 1))
        other = 1 - side[0]
        onward = lax.dynamic_index_in_dim(keep, other, 0, False) + lax.dynamic_index_in_dim(
            came, other, 0, False
        )
        return keep, came, lax.ppermute(onward, "query", swap_pairs(4, 2))

    first = [(0, 0, 0), (0, 1, 1), (0, 2, 2)]
    last = [(0, 3, 3), (1, 0, 4), (1, 1, 5), (1, 2, 6), (1, 3, 7)]
    u_first = projections(first, [grads], [u_factors, u_y, u_z], order, core)
    v_first = projections(first, [activations], [v_factors, v_y, v_z], order, core, u_first[:1])
    (near_first,) = block_scores(reduced(v_first), reduced(u_first), side, (near_position,))
    u_last = projections(last, [grads, g_in, g_out], [u_factors, u_y, u_z, u_d], order, core, (near_first,))
    v_last = projections(last, [activations, a_in, a_out], [v_factors, v_y, v_z, v_d], order, core, u_last[:1])
    near_slot = jnp.where(near_position >= 3 * capacity, near_position - 3 * capacity, -1)
    far_slot = jnp.where(far_position >= 0, far_position + capacity, -1)
    near_last, far = block_scores(reduced(v_last), reduced(u_last), side, (near_slot, far_slot))
    total = near_first + near_last + swap(far, mirror)
    return total.reshape(blocks, pick_count, total.shape[1])


def solution(mesh):
    placed = (P("dp", "query"), P("dp", "query"), P("query", "dp"), P("query", "dp"), P("dp", None))
    grid = mesh.shape["dp"] == 8 and mesh.shape["query"] == 4

    def step(*operands):
        if not grid:
            return exchange_plan(*operands)
        return mirror_plan(*operands)

    return jax.shard_map(
        step, mesh=mesh, in_specs=placed, out_specs=P("dp", None, "query"), check_vma=False
    )
```

```python
import jax
import jax.numpy as jnp
from jax import lax
from jax.experimental import pallas as pl
from jax.experimental.pallas import tpu as pltpu
from jax.sharding import PartitionSpec as P

R = 32
TOKENS_PER_BLOCK = 16
VMEM_BYTES = 64 * 2**20


def local_scores(received, v_factors, u_factors, reducer):
    recv_act, recv_grad = received
    peer_total, item_count, token_count, width_act = recv_act.shape
    row_total = peer_total * item_count * token_count
    flat_act = recv_act.reshape(row_total, width_act)
    flat_grad = recv_grad.reshape(row_total, recv_grad.shape[3])

    def partial_term(first_row, row_count):
        proj_act = lax.dot_general(
            v_factors, flat_act, (((0,), (1,)), ((), ())), preferred_element_type=jnp.float32
        )
        proj_grad = lax.dot_general(
            u_factors, flat_grad, (((0,), (1,)), ((), ())), preferred_element_type=jnp.float32
        )
        return jnp.stack([proj_act, proj_grad], axis=1)

    reduced = reducer(partial_term)
    products = reduced[:, 0] * reduced[:, 1]
    local_queries = products.shape[0] // R
    summed = jnp.sum(
        products.reshape(local_queries, R, peer_total, item_count, token_count), axis=(1, 4)
    )
    return jnp.transpose(summed, (1, 2, 0))


def exchange_plan(activations, grads, v_factors, u_factors, candidates):
    peer_total = lax.axis_size("dp")
    blocks = candidates.shape[0]
    pick_count = candidates.shape[1]
    token_count = activations.shape[0] // blocks
    capacity = 2 * blocks * pick_count // peer_total
    width_act = activations.shape[1]
    width_grad = grads.shape[1]
    column_total = v_factors.shape[1]
    local_rows = column_total // lax.axis_size("query")
    entry_total = blocks * pick_count
    slot_total = peer_total * capacity
    target = candidates.reshape(entry_total)
    onehot = (target[:, None] == jnp.arange(peer_total, dtype=jnp.int32)[None, :]).astype(jnp.int32)
    earlier = jnp.cumsum(onehot, axis=0) - onehot
    slot_index = jnp.sum(earlier * onehot, axis=1)
    position = target * capacity + slot_index
    matches = (position[None, :] == jnp.arange(slot_total, dtype=jnp.int32)[:, None]).astype(
        jnp.int32
    )
    owner_block = jnp.arange(entry_total, dtype=jnp.int32) // pick_count
    source = jnp.sum(matches * owner_block[None, :], axis=1)
    filled = jnp.sum(matches, axis=1) > 0
    act_blocks = activations.reshape(blocks, token_count, width_act)
    grad_blocks = grads.reshape(blocks, token_count, width_grad)
    send_act = jnp.where(
        filled[:, None, None],
        jnp.take(act_blocks, source, axis=0),
        jnp.zeros((), activations.dtype),
    )
    send_grad = jnp.where(
        filled[:, None, None], jnp.take(grad_blocks, source, axis=0), jnp.zeros((), grads.dtype)
    )
    send_act = send_act.reshape(peer_total, capacity, token_count, width_act)
    send_grad = send_grad.reshape(peer_total, capacity, token_count, width_grad)
    scored = local_scores(
        (
            lax.all_to_all(send_act, "dp", split_axis=0, concat_axis=0, tiled=True),
            lax.all_to_all(send_grad, "dp", split_axis=0, concat_axis=0, tiled=True),
        ),
        v_factors,
        u_factors,
        lambda partial_term: lax.psum_scatter(
            partial_term(jnp.int32(0), local_rows * lax.axis_size("query")),
            "query",
            scatter_dimension=0,
            tiled=True,
        ),
    )
    returned = lax.all_to_all(scored, "dp", split_axis=0, concat_axis=0, tiled=True)
    flattened = returned.reshape(slot_total, returned.shape[2])
    picked = jnp.take(flattened, position, axis=0)
    return picked.reshape(blocks, pick_count, returned.shape[2])


def swap_pairs(total, mask):
    return [(index, index ^ mask) for index in range(total)]


def grouped_products(units, sources, factors, order, flags, totals=None, bases=(), after=()):
    count = len(units)
    capacity = order.shape[1]
    width, columns = factors[0].shape
    token_count = TOKENS_PER_BLOCK
    rows = capacity * token_count
    part = rows // 2
    quarter = columns // 4
    queries = quarter // R
    dense = any(factor is None for _, factor, _ in units)
    first_total, own_total, partner_total, positions = totals if totals else (0, None, None, ())
    kinds = len(positions)
    held = len(sources) + len(factors) + len(after)
    added = [base for base in bases if base is not None]

    def body(order_ref, flags_ref, *refs):
        source_refs = refs[: len(sources)]
        factor_refs = refs[len(sources) : len(sources) + len(factors)]
        given = refs[held:]
        token_buffer, factor_buffer, product_buffer, sum_buffer, token_done, factor_done = refs[-6:]
        step = pl.program_id(0)
        first_core = flags_ref[0] == 0
        middle = flags_ref[1] == 1

        def factor_copy(which):
            return pltpu.make_async_copy(
                factor_refs[which], factor_buffer.at[which], factor_done.at[which]
            )

        def token_copy(origin, origin_row, unit, row, length):
            return pltpu.make_async_copy(
                origin.at[pl.ds(origin_row, length)],
                token_buffer.at[unit, pl.ds(row, length)],
                token_done.at[unit],
            )

        def fetch(unit):
            source, factor, first = units[unit]

            def gather(origin):
                for slot in range(capacity):
                    block = order_ref[first, slot]
                    token_copy(origin, block * token_count, unit, slot * token_count, token_count).start()

            if factor is None:
                inner, outer = source_refs[1], source_refs[-1]
                whole, end = sources[1].shape[0], sources[-1].shape[0]
                pl.when(middle)(lambda: token_copy(inner, whole - part, unit, 0, part).start())
                pl.when(jnp.logical_not(middle))(
                    lambda: token_copy(outer, end - part, unit, 0, part).start()
                )
            elif source == 0:
                gather(source_refs[0])
            else:
                pl.when(middle)(lambda: gather(source_refs[1]))
                pl.when(jnp.logical_not(middle))(lambda: gather(source_refs[2]))

        def give(unit, row, height, values):
            pieces = [values[:, place * quarter : (place + 1) * quarter] for place in range(4)]
            for side in range(2):
                even, odd = pieces[2 * side], pieces[2 * side + 1]
                span = pl.ds(row, height)
                if totals is None:
                    keep_ref, send_ref = given[:2]
                    keep_ref[side, span] = jnp.where(first_core, even, odd)
                    send_ref[side, span] = jnp.where(first_core, odd, even)
                else:
                    own, partner = given[0][side, span], given[1][side, span]
                    slots = pl.ds(unit * capacity + row // token_count, height // token_count)
                    for core, piece in enumerate((even, odd)):
                        total = jnp.where(first_core == (core == 0), own, partner)
                        product = (piece * total).reshape(height // token_count, token_count, quarter)
                        sum_buffer[2 * side + core, slots] = jnp.sum(product, axis=1)

        def times(unit, height, which):
            return jnp.dot(
                token_buffer[unit, :height], factor_buffer[which], preferred_element_type=jnp.float32
            )

        def compute(unit, fresh):
            _, factor, first = units[unit]
            height = part if factor is None else rows
            token_copy(source_refs[0], 0, unit, 0, height).wait()
            if factor is not None:
                if factor in fresh:
                    factor_copy(factor).wait()
                give(unit, 0, rows, times(unit, rows, factor))
                return
            for which in range(len(factors)):
                if which in fresh:
                    factor_copy(which).wait()
                product_buffer[which] = times(unit, part, which)
            for entry in range(capacity):
                which = order_ref[first, entry]
                row = entry // 2 * token_count
                product_buffer[len(factors) + entry // 8, entry % 8 * token_count : (entry % 8 + 1) * token_count] = (
                    product_buffer[which, row : row + token_count]
                )
            for half in range(2):
                give(unit, half * part, part, product_buffer[len(factors) + half])

        def finish():
            place = flags_ref[2]
            lane = lax.broadcasted_iota(jnp.int32, (4 * queries, quarter), 1)
            query = lax.broadcasted_iota(jnp.int32, (4 * queries, quarter), 0)
            sums = jnp.zeros((4 * queries, count * capacity), jnp.float32)
            for block in range(4):
                groups = jnp.where(lane // R + queries * block == query, 1.0, 0.0).astype(jnp.float32)
                sums = sums + lax.dot_general(
                    groups,
                    sum_buffer[block],
                    (((1,), (1,)), ((), ())),
                    precision=lax.Precision.HIGHEST,
                    preferred_element_type=jnp.float32,
                )
            position_refs = given[2 : 2 + kinds]
            base_refs = list(given[2 + kinds : 2 + kinds + len(added)])
            out_refs = given[2 + kinds + len(added) : 2 + kinds + len(added) + kinds]
            for kind in range(kinds):
                wanted = position_refs[kind][...]
                slot = lax.broadcasted_iota(jnp.int32, (count * capacity, wanted.shape[1]), 0)
                values = jnp.dot(
                    sums,
                    jnp.where(wanted == slot, 1.0, 0.0).astype(jnp.float32),
                    precision=lax.Precision.HIGHEST,
                    preferred_element_type=jnp.float32,
                )
                parts = [values[queries * block : queries * (block + 1)] for block in range(4)]
                base_ref = base_refs.pop(0) if bases[kind] is not None else None
                for offset in range(4):
                    mine = parts[offset]
                    for index in range(1, 4):
                        mine = jnp.where(place == index, parts[index ^ offset], mine)
                    if base_ref is not None:
                        mine = mine + base_ref[offset]
                    out_refs[kind][offset] = mine

        @pl.when(step == 0)
        def _():
            started = set()
            for unit, (source, factor, first) in enumerate(units):
                fetch(unit)
                for which in range(len(factors)) if factor is None else (factor,):
                    if which not in started:
                        started.add(which)
                        factor_copy(which).start()

        seen = set()
        for unit, (source, factor, first) in enumerate(units):
            used = set(range(len(factors))) if factor is None else {factor}
            pl.when(step == unit)(lambda unit=unit, fresh=used - seen: compute(unit, fresh))
            seen |= used
        if totals is not None:
            pl.when(step == count - 1)(finish)

    anywhere = pl.BlockSpec(memory_space=pltpu.HBM)
    scalars = pl.BlockSpec(memory_space=pltpu.SMEM)

    def whole(shape):
        return pl.BlockSpec(shape, lambda step: (0,) * len(shape))

    in_specs = [scalars, scalars] + [anywhere] * held
    operands = [order, flags, *sources, *factors, *after]
    if totals is None:
        result = jax.ShapeDtypeStruct((2, count * rows, quarter), jnp.float32)
        out_shape = (result, result)
        out_specs = (pl.BlockSpec((2, rows, quarter), lambda step: (0, step, 0)),) * 2
    else:
        shape = (4, queries, positions[0].shape[1])
        total_spec = pl.BlockSpec((2, rows, quarter), lambda step: (0, step + first_total, 0))
        in_specs += [total_spec] * 2 + [whole(positions[0].shape)] * kinds + [whole(shape)] * len(added)
        operands += [own_total, partner_total, *positions, *added]
        out_shape = (jax.ShapeDtypeStruct(shape, jnp.float32),) * kinds
        out_specs = (whole(shape),) * kinds
    return pl.pallas_call(
        body,
        grid=(count,),
        out_shape=out_shape,
        in_specs=in_specs,
        out_specs=out_specs,
        scratch_shapes=[
            pltpu.VMEM((count, rows, width), sources[0].dtype),
            pltpu.VMEM((len(factors), width, columns), factors[0].dtype),
            pltpu.VMEM((len(factors) + 2 if dense else 1, part, columns), jnp.float32),
            pltpu.VMEM((4, count * capacity, quarter), jnp.float32),
            pltpu.SemaphoreType.DMA((count,)),
            pltpu.SemaphoreType.DMA((len(factors),)),
        ],
        compiler_params=pltpu.CompilerParams(vmem_limit_bytes=VMEM_BYTES),
    )(*operands)


def slots_of(relative, pick_count, capacity):
    entries = relative.shape[0]
    onehot = (relative[:, None] == jnp.arange(4, dtype=jnp.int32)[None, :]).astype(jnp.int32)
    earlier = jnp.cumsum(onehot, axis=0) - onehot
    slot = jnp.sum(earlier * onehot, axis=1)
    position = jnp.where(relative < 4, relative * capacity + slot, -1)
    matches = position[None, :] == jnp.arange(4 * capacity, dtype=jnp.int32)[:, None]
    owner = jnp.arange(entries, dtype=jnp.int32) // pick_count
    order = jnp.sum(jnp.where(matches, owner[None, :], 0), axis=1)
    return order.reshape(4, capacity), position


def mirror_plan(activations, grads, v_factors, u_factors, candidates):
    me = lax.axis_index("dp")
    place = lax.axis_index("query")
    blocks, pick_count = candidates.shape
    entries = blocks * pick_count
    capacity = 2 * entries // 8
    late = capacity // 2
    early_rows = (blocks - late) * TOKENS_PER_BLOCK
    across_z = swap_pairs(8, 2)
    across_y = swap_pairs(8, 1)
    mirror = swap_pairs(8, 6)
    inner = mirror[2:6]
    outer = mirror[:2] + mirror[6:]
    is_inner = jnp.logical_and(me >= 2, me < 6).astype(jnp.int32)
    flags = jnp.stack([place % 2, is_inner, place])

    def swap(array, pairs, axis="dp"):
        return lax.ppermute(array, axis, pairs)

    grads_early, grads_late = grads[:early_rows], grads[early_rows:]
    acts_early, acts_late = activations[:early_rows], activations[early_rows:]
    mirrored = swap(candidates, mirror)
    u_y = swap(u_factors, across_y)
    u_z = swap(u_factors, across_z)
    v_y = swap(v_factors, across_y)
    v_z = swap(v_factors, across_z)
    g_in = swap(grads, inner)
    a_in = swap(activations, inner)
    g_out = swap(grads_early, outer)
    g_end = swap(grads_late, outer)
    a_out = swap(acts_early, outer)
    a_end = swap(acts_late, outer)
    u_d = swap(u_z, across_y)
    v_d = swap(v_z, across_y)

    three, four = 3 * capacity, 4 * capacity
    entry = jnp.arange(entries, dtype=jnp.int32)

    def placed(position, low, high, shift):
        chosen = jnp.logical_and(position >= low, position < high)
        return jnp.where(chosen, position + shift, -1).reshape(blocks, pick_count).T.reshape(1, entries)

    def summed(halves):
        keep, send = halves
        mine = keep + swap(send, swap_pairs(4, 1), "query")
        mine = mine + swap(mine, swap_pairs(4, 2), "query")
        return mine, swap(mine, swap_pairs(4, 1), "query")

    near_order, near_position = slots_of((candidates ^ me).reshape(entries), pick_count, capacity)
    near_three = placed(near_position, 0, three, 0)
    near_fourth = placed(near_position, three, four, -three)
    first = [(0, 0, 0), (0, 1, 1), (0, 2, 2)]
    slices = (grads_early, grads_late, acts_early, acts_late)
    u_first = grouped_products(first, [grads], [u_factors, u_y, u_z], near_order, flags, after=slices)
    g_first = summed(u_first)
    mirrored, _ = lax.optimization_barrier((mirrored, u_first[0]))
    far_relative = (mirrored ^ me).reshape(entries)
    is_late = entry >= entries - 2 * late
    far_order, far_position = slots_of(jnp.where(is_late, 4, far_relative), pick_count, capacity)
    end_order = jnp.minimum(far_relative[entries - 2 * late :], 3)
    order = jnp.concatenate([near_order, far_order, end_order[None]], axis=0)
    far_three = placed(far_position, 0, three, 0)
    far_fourth = placed(far_position, three, four, capacity - three)
    end_position = jnp.where(far_relative < 4, entry - (entries - 2 * late), -1)
    end_position = placed(end_position, 0, capacity, 0)

    (near,) = grouped_products(
        first,
        [activations],
        [v_factors, v_y, v_z],
        near_order,
        flags,
        totals=(0, *g_first, (near_three,)),
        bases=(None,),
    )
    straight = [(1, 0, 4), (1, 1, 5), (1, 2, 6)]
    u_far = grouped_products(
        straight, [grads, g_in, g_out], [u_factors, u_y, u_z], order, flags, after=(near, near_fourth, far_three, far_fourth, end_position)
    )
    g_far = summed(u_far)
    u_diagonal = grouped_products([(0, 0, 3), (1, 0, 7)], [grads, g_in, g_out], [u_d], order, flags, after=u_far[:1])
    g_diagonal = summed(u_diagonal)
    ending = [(1, None, 8)]
    u_end = grouped_products(
        ending, [grads, g_in, g_end], [u_factors, u_y, u_z, u_d], order, flags, after=u_diagonal[:1]
    )
    g_ending = summed(u_end)
    (far,) = grouped_products(
        straight,
        [activations, a_in, a_out],
        [v_factors, v_y, v_z],
        order,
        flags,
        totals=(0, *g_far, (far_three,)),
        bases=(None,),
        after=u_end[:1],
    )
    near, far = grouped_products(
        [(0, 0, 3), (1, 0, 7)],
        [activations, a_in, a_out],
        [v_d],
        order,
        flags,
        totals=(0, *g_diagonal, (near_fourth, far_fourth)),
        bases=(near, far),
    )
    (far,) = grouped_products(
        ending,
        [activations, a_in, a_end],
        [v_factors, v_y, v_z, v_d],
        order,
        flags,
        totals=(0, *g_ending, (end_position,)),
        bases=(far,),
        after=(near,),
    )
    partial = near + swap(far, mirror)
    total = partial[0]
    for offset in (1, 2, 3):
        total = total + swap(partial[offset], swap_pairs(4, offset), "query")
    return jnp.transpose(total.reshape(total.shape[0], pick_count, blocks), (2, 1, 0))


def solution(mesh):
    placed = (P("dp", "query"), P("dp", "query"), P("query", "dp"), P("query", "dp"), P("dp", None))
    grid = mesh.shape["dp"] == 8 and mesh.shape["query"] == 4

    def step(*operands):
        if not grid:
            return exchange_plan(*operands)
        return mirror_plan(*operands)

    return jax.shard_map(
        step, mesh=mesh, in_specs=placed, out_specs=P("dp", None, "query"), check_vma=False
    )
```

```python
import jax
import jax.numpy as jnp
from jax import lax
from jax.experimental import pallas as pl
from jax.experimental.pallas import tpu as pltpu
from jax.sharding import PartitionSpec as P

R = 32
TOKENS_PER_BLOCK = 16
VMEM_BYTES = 64 * 2**20


def local_scores(received, v_factors, u_factors, reducer):
    recv_act, recv_grad = received
    peer_total, item_count, token_count, width_act = recv_act.shape
    row_total = peer_total * item_count * token_count
    flat_act = recv_act.reshape(row_total, width_act)
    flat_grad = recv_grad.reshape(row_total, recv_grad.shape[3])

    def partial_term(first_row, row_count):
        proj_act = lax.dot_general(
            v_factors, flat_act, (((0,), (1,)), ((), ())), preferred_element_type=jnp.float32
        )
        proj_grad = lax.dot_general(
            u_factors, flat_grad, (((0,), (1,)), ((), ())), preferred_element_type=jnp.float32
        )
        return jnp.stack([proj_act, proj_grad], axis=1)

    reduced = reducer(partial_term)
    products = reduced[:, 0] * reduced[:, 1]
    local_queries = products.shape[0] // R
    summed = jnp.sum(
        products.reshape(local_queries, R, peer_total, item_count, token_count), axis=(1, 4)
    )
    return jnp.transpose(summed, (1, 2, 0))


def exchange_plan(activations, grads, v_factors, u_factors, candidates):
    peer_total = lax.axis_size("dp")
    blocks = candidates.shape[0]
    pick_count = candidates.shape[1]
    token_count = activations.shape[0] // blocks
    capacity = 2 * blocks * pick_count // peer_total
    width_act = activations.shape[1]
    width_grad = grads.shape[1]
    column_total = v_factors.shape[1]
    local_rows = column_total // lax.axis_size("query")
    entry_total = blocks * pick_count
    slot_total = peer_total * capacity
    target = candidates.reshape(entry_total)
    onehot = (target[:, None] == jnp.arange(peer_total, dtype=jnp.int32)[None, :]).astype(jnp.int32)
    earlier = jnp.cumsum(onehot, axis=0) - onehot
    slot_index = jnp.sum(earlier * onehot, axis=1)
    position = target * capacity + slot_index
    matches = (position[None, :] == jnp.arange(slot_total, dtype=jnp.int32)[:, None]).astype(
        jnp.int32
    )
    owner_block = jnp.arange(entry_total, dtype=jnp.int32) // pick_count
    source = jnp.sum(matches * owner_block[None, :], axis=1)
    filled = jnp.sum(matches, axis=1) > 0
    act_blocks = activations.reshape(blocks, token_count, width_act)
    grad_blocks = grads.reshape(blocks, token_count, width_grad)
    send_act = jnp.where(
        filled[:, None, None],
        jnp.take(act_blocks, source, axis=0),
        jnp.zeros((), activations.dtype),
    )
    send_grad = jnp.where(
        filled[:, None, None], jnp.take(grad_blocks, source, axis=0), jnp.zeros((), grads.dtype)
    )
    send_act = send_act.reshape(peer_total, capacity, token_count, width_act)
    send_grad = send_grad.reshape(peer_total, capacity, token_count, width_grad)
    scored = local_scores(
        (
            lax.all_to_all(send_act, "dp", split_axis=0, concat_axis=0, tiled=True),
            lax.all_to_all(send_grad, "dp", split_axis=0, concat_axis=0, tiled=True),
        ),
        v_factors,
        u_factors,
        lambda partial_term: lax.psum_scatter(
            partial_term(jnp.int32(0), local_rows * lax.axis_size("query")),
            "query",
            scatter_dimension=0,
            tiled=True,
        ),
    )
    returned = lax.all_to_all(scored, "dp", split_axis=0, concat_axis=0, tiled=True)
    flattened = returned.reshape(slot_total, returned.shape[2])
    picked = jnp.take(flattened, position, axis=0)
    return picked.reshape(blocks, pick_count, returned.shape[2])


def swap_pairs(total, mask):
    return [(index, index ^ mask) for index in range(total)]


def grouped_products(units, sources, factors, order, flags, totals=None, bases=(), after=()):
    count = len(units)
    capacity = order.shape[1]
    width, columns = factors[0].shape
    token_count = TOKENS_PER_BLOCK
    rows = capacity * token_count
    part = rows // 2
    quarter = columns // 4
    queries = quarter // R
    dense = any(factor is None for _, factor, _ in units)
    jobs, seen = [], set()
    for unit, (_, factor, _) in enumerate(units):
        for place, which in enumerate(range(len(factors)) if factor is None else (factor,)):
            jobs.append((unit, which, which not in seen, place == 0))
            seen.add(which)
    first_total, own_total, partner_total, positions = totals if totals else (0, None, None, ())
    kinds = len(positions)
    picks = 2
    held = len(sources) + len(factors) + len(after)
    added = [base for base in bases if base is not None]

    def body(order_ref, flags_ref, *refs):
        source_refs = refs[: len(sources)]
        factor_refs = refs[len(sources) : len(sources) + len(factors)]
        given = refs[held:]
        token_buffer, factor_buffer, product_buffer, sum_buffer, total_buffer = refs[-8:-3]
        token_done, factor_done, total_done = refs[-3:]
        step = pl.program_id(0)
        first_core = flags_ref[0] == 0
        middle = flags_ref[1] == 1

        def factor_copy(which):
            return pltpu.make_async_copy(
                factor_refs[which], factor_buffer.at[which], factor_done.at[which]
            )

        def token_copy(origin, origin_row, unit, row, length):
            return pltpu.make_async_copy(
                origin.at[pl.ds(origin_row, length)],
                token_buffer.at[unit, pl.ds(row, length)],
                token_done.at[unit],
            )

        def total_copy(unit, kind):
            return pltpu.make_async_copy(
                given[kind].at[:, pl.ds((first_total + unit) * rows, rows)],
                total_buffer.at[unit, kind],
                total_done.at[unit, kind],
            )

        def fetch(unit):
            source, factor, first = units[unit]

            def gather(origin):
                for slot in range(capacity):
                    block = order_ref[first, slot]
                    token_copy(origin, block * token_count, unit, slot * token_count, token_count).start()

            if factor is None:
                inner, outer = source_refs[1], source_refs[-1]
                whole, end = sources[1].shape[0], sources[-1].shape[0]
                pl.when(middle)(lambda: token_copy(inner, whole - part, unit, 0, part).start())
                pl.when(jnp.logical_not(middle))(
                    lambda: token_copy(outer, end - part, unit, 0, part).start()
                )
            elif source == 0:
                gather(source_refs[0])
            else:
                pl.when(middle)(lambda: gather(source_refs[1]))
                pl.when(jnp.logical_not(middle))(lambda: gather(source_refs[2]))

        def give(unit, row, height, values):
            pieces = [values[:, place * quarter : (place + 1) * quarter] for place in range(4)]
            for side in range(2):
                even, odd = pieces[2 * side], pieces[2 * side + 1]
                span = pl.ds(row, height)
                if totals is None:
                    keep_ref, send_ref = given[:2]
                    keep_ref[side, span] = jnp.where(first_core, even, odd)
                    send_ref[side, span] = jnp.where(first_core, odd, even)
                else:
                    own, partner = (total_buffer[unit, kind, side, span] for kind in range(2))
                    slots = pl.ds(unit * capacity + row // token_count, height // token_count)
                    for core, piece in enumerate((even, odd)):
                        total = jnp.where(first_core == (core == 0), own, partner)
                        product = (piece * total).reshape(height // token_count, token_count, quarter)
                        sum_buffer[2 * side + core, slots] = jnp.sum(product, axis=1)

        def times(unit, height, which):
            return jnp.dot(
                token_buffer[unit, :height], factor_buffer[which], preferred_element_type=jnp.float32
            )

        def wait_totals(unit):
            if totals is not None:
                for kind in range(2):
                    total_copy(unit, kind).wait()

        def issue(index):
            if index < len(jobs):
                unit, which, fresh, opens = jobs[index]
                if opens:
                    fetch(unit)
                if fresh:
                    factor_copy(which).start()
                if opens and totals is not None:
                    for kind in range(2):
                        total_copy(unit, kind).start()

        def compute(unit):
            _, factor, first = units[unit]
            height = part if factor is None else rows
            for index, (owner, which, fresh, opens) in enumerate(jobs):
                if owner != unit:
                    continue
                if opens:
                    token_copy(source_refs[0], 0, unit, 0, height).wait()
                if fresh:
                    factor_copy(which).wait()
                issue(index + 2)
                product = times(unit, height, which)
                if factor is None:
                    product_buffer[which] = product
            wait_totals(unit)
            if factor is not None:
                give(unit, 0, rows, product)
                return
            half = capacity // 2
            for entry in range(capacity):
                which = order_ref[first, entry]
                row = entry // 2 * token_count
                target = entry % half * token_count
                product_buffer[len(factors) + entry // half, target : target + token_count] = (
                    product_buffer[which, row : row + token_count]
                )
            for half in range(2):
                give(unit, half * part, part, product_buffer[len(factors) + half])

        def finish():
            place = flags_ref[2]
            lane = lax.broadcasted_iota(jnp.int32, (4 * queries, quarter), 1)
            query = lax.broadcasted_iota(jnp.int32, (4 * queries, quarter), 0)
            sums = jnp.zeros((4 * queries, count * capacity), jnp.float32)
            for block in range(4):
                groups = jnp.where(lane // R + queries * block == query, 1.0, 0.0).astype(jnp.float32)
                sums = sums + lax.dot_general(
                    groups,
                    sum_buffer[block],
                    (((1,), (1,)), ((), ())),
                    precision=lax.Precision.HIGHEST,
                    preferred_element_type=jnp.float32,
                )
            position_refs = given[2 : 2 + kinds]
            base_refs = list(given[2 + kinds : 2 + kinds + len(added)])
            out_refs = given[2 + kinds + len(added) : 2 + kinds + len(added) + kinds]
            for kind in range(kinds):
                wanted = position_refs[kind][...]
                slot = lax.broadcasted_iota(jnp.int32, (count * capacity, wanted.shape[1]), 0)
                values = jnp.dot(
                    sums,
                    jnp.where(wanted == slot, 1.0, 0.0).astype(jnp.float32),
                    precision=lax.Precision.HIGHEST,
                    preferred_element_type=jnp.float32,
                )
                parts = [values[queries * block : queries * (block + 1)] for block in range(4)]
                base_ref = base_refs.pop(0) if bases[kind] is not None else None
                for offset in range(4):
                    mine = parts[offset]
                    for index in range(1, 4):
                        mine = jnp.where(place == index, parts[index ^ offset], mine)
                    for pick in range(picks):
                        piece = mine[:, pick * (mine.shape[1] // picks) : (pick + 1) * (mine.shape[1] // picks)]
                        if base_ref is not None:
                            piece = piece + base_ref[offset, pick]
                        out_refs[kind][offset, pick] = piece

        @pl.when(step == 0)
        def _():
            issue(0)
            issue(1)

        for unit in range(count):
            if totals is not None:
                compute(unit)
            else:
                pl.when(step == unit)(lambda unit=unit: compute(unit))
        if totals is not None:
            finish()

    anywhere = pl.BlockSpec(memory_space=pltpu.HBM)
    scalars = pl.BlockSpec(memory_space=pltpu.SMEM)

    def whole(shape):
        return pl.BlockSpec(shape, lambda step: (0,) * len(shape))

    in_specs = [scalars, scalars] + [anywhere] * held
    operands = [order, flags, *sources, *factors, *after]
    if totals is None:
        result = jax.ShapeDtypeStruct((2, count * rows, quarter), jnp.float32)
        out_shape = (result, result)
        out_specs = (pl.BlockSpec((2, rows, quarter), lambda step: (0, step, 0)),) * 2
    else:
        shape = (4, picks, queries, positions[0].shape[1] // picks)
        in_specs += [anywhere] * 2 + [whole(positions[0].shape)] * kinds + [whole(shape)] * len(added)
        operands += [own_total, partner_total, *positions, *added]
        out_shape = (jax.ShapeDtypeStruct(shape, jnp.float32),) * kinds
        out_specs = (whole(shape),) * kinds
    return pl.pallas_call(
        body,
        grid=(count if totals is None else 1,),
        out_shape=out_shape,
        in_specs=in_specs,
        out_specs=out_specs,
        scratch_shapes=[
            pltpu.VMEM((count, rows, width), sources[0].dtype),
            pltpu.VMEM((len(factors), width, columns), factors[0].dtype),
            pltpu.VMEM((len(factors) + 2 if dense else 1, part, columns), jnp.float32),
            pltpu.VMEM((4, count * capacity, quarter), jnp.float32),
            pltpu.VMEM((count if totals else 1, 2, 2, rows, quarter), jnp.float32),
            pltpu.SemaphoreType.DMA((count,)),
            pltpu.SemaphoreType.DMA((len(factors),)),
            pltpu.SemaphoreType.DMA((count, 2)),
        ],
        compiler_params=pltpu.CompilerParams(vmem_limit_bytes=VMEM_BYTES),
    )(*operands)


def slots_of(relative, pick_count, capacity):
    entries = relative.shape[0]
    onehot = (relative[:, None] == jnp.arange(4, dtype=jnp.int32)[None, :]).astype(jnp.int32)
    earlier = jnp.cumsum(onehot, axis=0) - onehot
    slot = jnp.sum(earlier * onehot, axis=1)
    position = jnp.where(relative < 4, relative * capacity + slot, -1)
    matches = position[None, :] == jnp.arange(4 * capacity, dtype=jnp.int32)[:, None]
    owner = jnp.arange(entries, dtype=jnp.int32) // pick_count
    order = jnp.sum(jnp.where(matches, owner[None, :], 0), axis=1)
    return order.reshape(4, capacity), position


def mirror_plan(activations, grads, v_factors, u_factors, candidates):
    me = lax.axis_index("dp")
    place = lax.axis_index("query")
    blocks, pick_count = candidates.shape
    entries = blocks * pick_count
    capacity = 2 * entries // 8
    late = 3 * blocks // 8
    early_rows = (blocks - late) * TOKENS_PER_BLOCK
    across_z = swap_pairs(8, 2)
    across_y = swap_pairs(8, 1)
    mirror = swap_pairs(8, 6)
    inner = mirror[2:6]
    outer = mirror[:2] + mirror[6:]
    is_inner = jnp.logical_and(me >= 2, me < 6).astype(jnp.int32)
    flags = jnp.stack([place % 2, is_inner, place])

    def swap(array, pairs, axis="dp"):
        return lax.ppermute(array, axis, pairs)

    grads_early, grads_late = grads[:early_rows], grads[early_rows:]
    acts_early, acts_late = activations[:early_rows], activations[early_rows:]
    mirrored = swap(candidates, mirror)
    u_y = swap(u_factors, across_y)
    u_z = swap(u_factors, across_z)
    v_y = swap(v_factors, across_y)
    v_z = swap(v_factors, across_z)
    g_in = swap(grads, inner)
    a_in = swap(activations, inner)
    g_out = swap(grads_early, outer)
    g_end = swap(grads_late, outer)
    a_out = swap(acts_early, outer)
    a_end = swap(acts_late, outer)
    u_d = swap(u_z, across_y)
    v_d = swap(v_z, across_y)

    three, four = 3 * capacity, 4 * capacity
    entry = jnp.arange(entries, dtype=jnp.int32)

    def placed(position, low, high, shift):
        chosen = jnp.logical_and(position >= low, position < high)
        return jnp.where(chosen, position + shift, -1).reshape(blocks, pick_count).T.reshape(1, entries)

    def summed(halves):
        keep, send = halves
        mine = keep + swap(send, swap_pairs(4, 1), "query")
        mine = mine + swap(mine, swap_pairs(4, 2), "query")
        return mine, swap(mine, swap_pairs(4, 1), "query")

    near_order, near_position = slots_of((candidates ^ me).reshape(entries), pick_count, capacity)
    near_three = placed(near_position, 0, three, 0)
    near_fourth = placed(near_position, three, four, -three)
    first = [(0, 0, 0), (0, 1, 1), (0, 2, 2)]
    slices = (grads_early, grads_late, acts_early, acts_late)
    u_first = grouped_products(first, [grads], [u_factors, u_y, u_z], near_order, flags, after=slices)
    g_first = summed(u_first)
    mirrored, _ = lax.optimization_barrier((mirrored, u_first[0]))
    far_relative = (mirrored ^ me).reshape(entries)
    is_late = entry >= entries - 2 * late
    far_order, far_position = slots_of(jnp.where(is_late, 4, far_relative), pick_count, capacity)
    end_order = jnp.minimum(far_relative[entries - 2 * late :], 3)
    end_order = end_order[None]
    order = jnp.concatenate([near_order, far_order], axis=0)
    far_three = placed(far_position, 0, three, 0)
    far_fourth = placed(far_position, three, four, capacity - three)
    end_position = jnp.where(far_relative < 4, entry - (entries - 2 * late), -1)
    end_position = placed(end_position, 0, 2 * late, 0)

    (near,) = grouped_products(
        first,
        [activations],
        [v_factors, v_y, v_z],
        near_order,
        flags,
        totals=(0, *g_first, (near_three,)),
        bases=(None,),
    )
    straight = [(1, 0, 4), (1, 1, 5), (1, 2, 6)]
    u_far = grouped_products(
        straight, [grads, g_in, g_out], [u_factors, u_y, u_z], order, flags, after=(near, near_fourth, far_three, far_fourth, end_position, end_order)
    )
    g_far = summed(u_far)
    u_diagonal = grouped_products([(0, 0, 3), (1, 0, 7)], [grads, g_in, g_out], [u_d], order, flags, after=u_far[:1])
    g_diagonal = summed(u_diagonal)
    ending = [(1, None, 0)]
    u_end = grouped_products(
        ending, [grads, g_in, g_end], [u_factors, u_y, u_z, u_d], end_order, flags, after=u_diagonal[:1]
    )
    g_ending = summed(u_end)
    (far,) = grouped_products(
        straight,
        [activations, a_in, a_out],
        [v_factors, v_y, v_z],
        order,
        flags,
        totals=(0, *g_far, (far_three,)),
        bases=(None,),
        after=u_end[:1],
    )
    near, far = grouped_products(
        [(0, 0, 3), (1, 0, 7)],
        [activations, a_in, a_out],
        [v_d],
        order,
        flags,
        totals=(0, *g_diagonal, (near_fourth, far_fourth)),
        bases=(near, far),
    )
    (far,) = grouped_products(
        ending,
        [activations, a_in, a_end],
        [v_factors, v_y, v_z, v_d],
        end_order,
        flags,
        totals=(0, *g_ending, (end_position,)),
        bases=(far,),
        after=(near,),
    )
    partial = near + swap(far, mirror)
    total = partial[0]
    for offset in (1, 2, 3):
        total = total + swap(partial[offset], swap_pairs(4, offset), "query")
    return jnp.transpose(total, (2, 0, 1))


def solution(mesh):
    placed = (P("dp", "query"), P("dp", "query"), P("query", "dp"), P("query", "dp"), P("dp", None))
    grid = mesh.shape["dp"] == 8 and mesh.shape["query"] == 4

    def step(*operands):
        if not grid:
            return exchange_plan(*operands)
        return mirror_plan(*operands)

    return jax.shard_map(
        step, mesh=mesh, in_specs=placed, out_specs=P("dp", None, "query"), check_vma=False
    )
```
